32 devices in a mesh: row: 2 (over core), col: 4 (over z), ind: 4 (over y, x).
Axes of the slice: x: 2, y: 2, z: 4, core: 2. Of those that a mesh axis runs over, the one named last changes fastest.
Arguments:
- dosages: bfloat16 [4096, 1024], P('ind', ('row', 'col'))
- annotations: bfloat16 [1024, 1024], P('ind', ('row', 'col')), may hold values from -6 to 6
- window_end: int32 [1024], P(('row', 'col')), may hold values from 512 to 1024, as said below
Outputs:
- ld_scores: float32 [1024, 1024], P('ind', ('row', 'col'))
The draws below stay inside these ranges and needn't reach their ends.
Inputs may be any that keep to these rules, and one draw needn't show every extreme that they name: window_end is nondecreasing, window_end[j] > j, and window_end[j] <= min(1024, (j // 128 + 4) * 128), the last bound reached in every draw.
All inputs are finite; a program needn't handle non-finite values.
Results may differ from the reference program's by a relative error of at most 0.0029.
Values may be sent and summed in bfloat16 or wider, within the bound.
A program may use at most 64 MiB of HBM per device.

```python
import jax
import jax.numpy as jnp
from jax import lax

ANNOT = 1024
TILE = 128
INDIV = 4096
VARIANTS = 1024
N_COL = 4


def draw_dosages(key, part):
    keys = jax.random.split(key, 5)
    phase_count = 32
    factor_span = 4 * N_COL * TILE
    stride = factor_span // phase_count
    factor_blocks = VARIANTS // factor_span + 2
    noise = jax.random.normal(keys[0], (INDIV, VARIANTS), jnp.float32)
    factors = jax.random.normal(keys[1], (phase_count, INDIV, factor_blocks), jnp.float32)
    local = jnp.repeat(jax.random.normal(keys[2], (INDIV, VARIANTS // 16), jnp.float32), 16, axis=1)
    load_local = jax.random.uniform(keys[3], (VARIANTS,), jnp.float32, 0.15, 0.35)
    loads = 0.114 * jax.random.uniform(keys[4], (phase_count, VARIANTS), jnp.float32, 0.2, 1.8)
    position = jnp.arange(VARIANTS, dtype=jnp.int32)
    mixed = 0.7 * noise + load_local * local
    for phase in range(phase_count):
        which = (position + phase * stride) // factor_span
        spread = jnp.take(factors[phase], which, axis=1)
        mixed = mixed + loads[phase] * spread
    return mixed.astype(jnp.bfloat16)


def draw_window_end(key, part):
    keys = jax.random.split(key, 2)
    spacing = jax.random.randint(keys[0], (VARIANTS,), 1, 10)
    dense = jax.random.randint(keys[1], (VARIANTS // 16,), 0, 4) == 0
    dense = jnp.repeat(dense, 16)
    position = jnp.arange(VARIANTS, dtype=jnp.int32)
    dense = dense | (position < TILE * N_COL)
    spacing = jnp.where(dense, 1, spacing).astype(jnp.int32)
    centimorgan = jnp.cumsum(spacing).astype(jnp.int32)
    reach = 3 * TILE * N_COL
    found = jnp.searchsorted(centimorgan, centimorgan + reach, side='right').astype(jnp.int32)
    bound = (position // TILE + N_COL) * TILE
    return jnp.minimum(jnp.minimum(found, bound), VARIANTS).astype(jnp.int32)


def shard_levels(rng, extent, cuts, least, largest):
    factor_of, own = 1.0, jax.random.fold_in(rng, 6)
    for dim, shards_of in cuts:
        heights = jnp.exp(jax.random.uniform(jax.random.fold_in(own, dim), (shards_of,), jnp.float32, least / len(cuts), largest / len(cuts)))
        factor_of = factor_of * jnp.repeat(heights, extent[dim] // shards_of).reshape([-1 if axis == dim else 1 for axis in range(len(extent))])
    return factor_of


def scatter_about(own_key, shape, scale, most, shards=(), held_as=jnp.bfloat16):
    result = scale * jax.random.normal(own_key, shape, jnp.float32)
    if shards:
        result = result * shard_levels(own_key, shape, shards, -0.22, 0.18)
    return jnp.clip(result, -most, most).astype(held_as)


def setup_inputs(seed: int = 0) -> dict:
    splits = jax.random.split(jax.random.key(seed), 4)
    return {
        "dosages": draw_dosages(jax.random.fold_in(splits[3], 71), 0),
        "annotations": scatter_about(splits[1], (ANNOT, VARIANTS), 1.0, 6.0, ((0, 4), (1, 8))),
        "window_end": draw_window_end(jax.random.fold_in(splits[3], 71), 0),
    }


def reference(dosages, annotations, window_end):
    variant_count = dosages.shape[1]
    sample_count = dosages.shape[0]
    span = N_COL * TILE
    padded_x = jnp.pad(dosages, ((0, 0), (0, span)))
    padded_a = jnp.pad(annotations, ((0, 0), (0, span)))
    total = jnp.zeros((annotations.shape[0], variant_count + span), jnp.float32)
    row_local = jnp.arange(TILE, dtype=jnp.int32)[:, None]
    col_local = jnp.arange(span, dtype=jnp.int32)[None, :]

    def step(acc, block):
        start = (block * TILE).astype(jnp.int32)
        rows_x = lax.dynamic_slice_in_dim(padded_x, start, TILE, 1)
        cols_x = lax.dynamic_slice_in_dim(padded_x, start, span, 1)
        gram = jnp.dot(rows_x.T, cols_x, preferred_element_type=jnp.float32)
        correlation_matrix = gram / sample_count
        raw_rsquared = correlation_matrix * correlation_matrix
        unbiased_rsquared = raw_rsquared - (1.0 - raw_rsquared) / (sample_count - 2)
        row_pos = start + row_local
        col_pos = start + col_local
        limit = lax.dynamic_slice_in_dim(window_end, start, TILE)[:, None]
        inside = col_pos < limit
        upper = jnp.where((col_pos >= row_pos) & inside, unbiased_rsquared, 0.0).astype(jnp.bfloat16)
        strict = jnp.where((col_pos > row_pos) & inside, unbiased_rsquared, 0.0).astype(jnp.bfloat16)
        annotation_rows = lax.dynamic_slice_in_dim(padded_a, start, TILE, 1)
        cols_a = lax.dynamic_slice_in_dim(padded_a, start, span, 1)
        direct = jnp.dot(cols_a, upper.T, preferred_element_type=jnp.float32)
        mirror = jnp.dot(annotation_rows, strict, preferred_element_type=jnp.float32)
        own_part = lax.dynamic_slice_in_dim(acc, start, TILE, 1) + direct
        acc = lax.dynamic_update_slice_in_dim(acc, own_part, start, 1)
        far_part = lax.dynamic_slice_in_dim(acc, start, span, 1) + mirror
        acc = lax.dynamic_update_slice_in_dim(acc, far_part, start, 1)
        return acc, None

    blocks = jnp.arange(variant_count // TILE, dtype=jnp.int32)
    total, unused = lax.scan(step, total, blocks)
    return total[:, :variant_count]
```

```python
import functools

import jax
import jax.numpy as jnp
from jax import lax
from jax.experimental import pallas as pl
from jax.experimental.pallas import tpu as pltpu
from jax.sharding import PartitionSpec as P

MESH = pl.DeviceIdType.MESH


def kernel(rows, cols, inds, samples, x_ref, a_ref, w_ref, o_ref, xs, xn, xt, nt, wl, wc,
           gp, rs, sq, sm, am, sems):
    (load_sem, xsend, xrecv, nsend, nrecv, wsend, wrecv, aup, adn, axs, arecv, crecv,
     rsend, rrecv, ssend, srecv) = sems
    r, c, i = lax.axis_index("row"), lax.axis_index("col"), lax.axis_index("ind")
    tile = x_ref.shape[1]
    part = tile // inds
    last = r == rows - 1
    toward = jnp.where(last, -1, 1)
    arrivals = jnp.where(last, c, cols - 1 - c)
    nxt = c - toward
    has_next = (nxt >= 0) & (nxt < cols)
    has_row_below = r < rows - 1
    has_row_above = r > 0

    def dev(row, col, ind):
        return {"row": row, "col": col, "ind": ind}

    def remote(src, dst, send, recv, target):
        return pltpu.make_async_remote_copy(
            src_ref=src, dst_ref=dst, send_sem=send, recv_sem=recv,
            device_id=target, device_id_type=MESH)

    def when(cond, fn):
        pl.when(cond)(fn)

    def loop(lo, hi, fn):
        def body(step, carry):
            fn(step)
            return carry
        lax.fori_loop(lo, hi, body, 0)

    barrier = pltpu.get_barrier_semaphore()

    def greet(row, col, ind):
        pl.semaphore_signal(barrier, inc=1, device_id=dev(row, col, ind), device_id_type=MESH)

    def greet_col(col):
        def each(k):
            ind = lax.rem(i + k, inds)
            when((col != c) | (k > 0), lambda: greet(r, col, ind))
            when((col < c) & has_row_below, lambda: greet(r + 1, col, ind))
            when((col > c) & has_row_above, lambda: greet(r - 1, col, ind))
            when((col == c) & has_row_below, lambda: greet(r + 1, col, ind))
            when((col == c) & has_row_above, lambda: greet(r - 1, col, ind))
        loop(0, inds, each)

    loop(0, cols, greet_col)
    below = has_row_below.astype(jnp.int32)
    above = has_row_above.astype(jnp.int32)
    peers = cols + below * (c + 1) + above * (cols - c)
    pl.semaphore_wait(barrier, peers * inds - 1)

    def send_x(slot, src):
        return remote(src, xs.at[slot + 1], xsend.at[slot], xrecv.at[slot + 1], dev(r, nxt, i))

    send_up_row = remote(x_ref, xn, nsend.at[0], nrecv.at[0], dev(r - 1, c, i))

    def send_w(step):
        return remote(w_ref, wl.at[c], wsend.at[step], wrecv.at[c],
                      dev(r, c - toward * step, i))

    def a_up(col, src):
        return remote(src, am.at[0, col], aup.at[col], arecv.at[col], dev(r, c + 1, i))

    def a_down(col, src):
        return remote(src, am.at[0, col], adn.at[col], arecv.at[col], dev(r, c - 1, i))

    def a_cross(col, row):
        return remote(am.at[0, col], am.at[1, col], axs.at[col], crecv.at[col], dev(row, c, i))

    when(has_next, lambda: send_x(0, x_ref).start())
    when(has_row_above, lambda: send_up_row.start())
    load_x = pltpu.make_async_copy(x_ref, xs.at[0], load_sem.at[0])
    load_x.start()
    load_a = pltpu.make_async_copy(a_ref, am.at[0, c], load_sem.at[1])
    load_a.start()
    w_count = cols - 1 - arrivals
    loop(1, w_count + 1, lambda step: send_w(step).start())
    when(c + 1 < cols, lambda: a_up(c, a_ref).start())
    when(c > 0, lambda: a_down(c, a_ref).start())

    w_own = w_ref[...]
    wl[c] = w_own
    wide = jnp.broadcast_to(w_own.astype(jnp.float32), (tile, tile))
    wc[...] = wide.T.astype(jnp.int32).reshape(inds, part, tile)

    def reduce_send(t, k):
        to = lax.rem(i + k, inds)
        return remote(gp.at[t, to], rs.at[k - 1, t], rsend.at[k - 1, t], rrecv.at[k - 1, t],
                      dev(r, c, to))

    def put_tile(t, value):
        gp[t] = value.reshape(inds, part, tile)
        loop(1, inds, lambda k: reduce_send(t, k).start())

    load_x.wait()
    xt[...] = xs[0].T
    put_tile(0, jnp.dot(xt[...], xs[0], preferred_element_type=jnp.float32))

    def take_next_row():
        send_up_row.wait_recv()
        nt[...] = xn[...].T

    when(has_row_below, take_next_row)

    row_iota = lax.broadcasted_iota(jnp.int32, (part, tile), 0) + i * part
    lane_iota = lax.broadcasted_iota(jnp.int32, (part, tile), 1)

    def s_send(t, which, k, kind, row, col, slot):
        to = lax.rem(i + k, inds)
        return remote(sq.at[t], sm.at[kind, slot, i], ssend.at[t, which, k],
                      srecv.at[kind, slot, i], dev(row, col, to))

    def total_of(t):
        total = gp[t, i]
        for k in range(1, inds):
            reduce_send(t, k).wait_recv()
            total = total + rs[k - 1, t]
        corr = total / samples
        rsq = corr * corr
        return rsq - (1.0 - rsq) / (samples - 2)

    def finish_diag():
        adj = total_of(0)
        base = (r * cols + c) * tile
        ahead = lane_iota >= row_iota
        pos = base + jnp.where(ahead, lane_iota, row_iota)
        lim = jnp.where(ahead, wc[i], jnp.broadcast_to(wl[c], (part, tile)))
        val = jnp.where(pos < lim, adj, 0.0).astype(jnp.bfloat16)
        sq[0] = val
        sm[0, c, i] = val
        loop(1, inds, lambda k: s_send(0, 0, k, 0, r, c, c).start())

    def finish_same(s):
        col = c + toward * s
        adj = total_of(s)
        pos = jnp.where(last, (r * cols + c) * tile + row_iota, (r * cols + col) * tile + lane_iota)
        lim = jnp.where(last, jnp.broadcast_to(wl[col], (part, tile)), wc[i])
        val = jnp.where(pos < lim, adj, 0.0).astype(jnp.bfloat16)
        sq[s] = val
        sm[0, col, i] = val
        loop(0, inds, lambda k: s_send(s, 1, k, 0, r, col, c).start())
        loop(1, inds, lambda k: s_send(s, 0, k, 0, r, c, col).start())

    def finish_cross(s):
        col = c + toward * s
        t = cols - 1 + s
        adj = total_of(t)
        pos = ((r + 1) * cols + c) * tile + row_iota
        lim = jnp.broadcast_to(wl[col], (part, tile))
        sq[t] = jnp.where(pos < lim, adj, 0.0).astype(jnp.bfloat16)
        loop(0, inds, lambda k: s_send(t, 1, k, 1, r, col, c).start())
        loop(0, inds, lambda k: s_send(t, 0, k, 1, r + 1, c, col).start())

    def finish(s):
        col = c + toward * s
        remote(w_ref, wl.at[col], wsend.at[0], wrecv.at[col], dev(r, nxt, i)).wait_recv()
        finish_same(s)
        when(has_row_below, lambda: finish_cross(s))

    def pass_a(s):
        def from_below():
            col = c - s
            a_up(col, am.at[0, col]).wait_recv()
            when(c + 1 < cols, lambda: a_up(col, am.at[0, col]).start())
            when(has_row_above, lambda: a_cross(col, r - 1).start())

        def from_above():
            col = c + s
            a_down(col, am.at[0, col]).wait_recv()
            when(c > 0, lambda: a_down(col, am.at[0, col]).start())
            when(has_row_below, lambda: a_cross(col, r + 1).start())

        when(c - s >= 0, from_below)
        when(c + s < cols, from_above)

    def step_x(s):
        send_x(s - 1, xs.at[s - 1]).wait_recv()
        when(has_next, lambda: send_x(s, xs.at[s]).start())
        put_tile(s, jnp.dot(xt[...], xs[s], preferred_element_type=jnp.float32))
        when(has_row_below, lambda: put_tile(
            cols - 1 + s, jnp.dot(nt[...], xs[s], preferred_element_type=jnp.float32)))

    def step(s):
        when(s <= arrivals, lambda: step_x(s))
        pass_a(s)
        when(s == 1, finish_diag)
        when((s >= 2) & (s - 1 <= arrivals), lambda: finish(s - 1))

    loop(1, cols, step)
    when(arrivals == cols - 1, lambda: finish(cols - 1))

    load_a.wait()

    def take(kind, slot, q):
        remote(sq.at[0], sm.at[kind, slot, q], ssend.at[0, 0, 0], srecv.at[kind, slot, q],
               dev(r, c, lax.rem(i + 1, inds))).wait_recv()

    def add(kind, slot, flip):
        lhs = am[kind, slot]
        rhs = sm[kind, slot].reshape(tile, tile)
        dims = (((1,), (1,)), ((), ())) if flip else (((1,), (0,)), ((), ()))
        o_ref[...] += lax.dot_general(lhs, rhs, dims, preferred_element_type=jnp.float32)

    loop(1, inds, lambda k: take(0, c, lax.rem(i + k, inds)))
    o_ref[...] = lax.dot_general(am[0, c], sm[0, c].reshape(tile, tile),
                                 (((1,), (0,)), ((), ())), preferred_element_type=jnp.float32)

    def add_home(s):
        col = c + toward * s
        loop(1, inds, lambda k: take(0, col, lax.rem(i + k, inds)))
        add(0, col, True)

    loop(1, arrivals + 1, add_home)

    def add_away(s):
        col = c - toward * s
        loop(0, inds, lambda q: take(0, col, q))
        add(0, col, False)

    loop(1, w_count + 1, add_away)

    def add_cross(col):
        a_cross_wait = remote(am.at[0, col], am.at[1, col], axs.at[col], crecv.at[col],
                              dev(r, nxt, i))
        a_cross_wait.wait_recv()
        loop(0, inds, lambda q: take(1, col, q))
        when(col < c, lambda: add(1, col, False))
        when(col > c, lambda: add(1, col, True))

    when(has_row_below, lambda: loop(0, c, add_cross))
    when(has_row_above, lambda: loop(c + 1, cols, add_cross))

    when(has_next, lambda: loop(0, arrivals + 1, lambda s: send_x(s, xs.at[s]).wait_send()))
    when(has_row_above, lambda: send_up_row.wait_send())
    loop(1, w_count + 1, lambda s: send_w(s).wait_send())
    when(c + 1 < cols, lambda: loop(0, c + 1, lambda q: a_up(q, am.at[0, q]).wait_send()))
    when(c > 0, lambda: loop(c, cols, lambda q: a_down(q, am.at[0, q]).wait_send()))
    when(has_row_above, lambda: loop(0, c, lambda q: a_cross(q, r - 1).wait_send()))
    when(has_row_below, lambda: loop(c + 1, cols, lambda q: a_cross(q, r + 1).wait_send()))

    def drain(t, kind, row, col):
        loop(1, inds, lambda k: reduce_send(t, k).wait_send())
        loop(0, inds, lambda k: s_send(t, 1, k, kind, r, col, c).wait_send())

    loop(1, inds, lambda k: reduce_send(0, k).wait_send())
    loop(1, inds, lambda k: s_send(0, 0, k, 0, r, c, c).wait_send())

    def drain_step(s):
        col = c + toward * s
        drain(s, 0, r, col)
        loop(1, inds, lambda k: s_send(s, 0, k, 0, r, c, col).wait_send())

        def cross():
            drain(cols - 1 + s, 1, r, col)
            loop(0, inds, lambda k: s_send(cols - 1 + s, 0, k, 1, r + 1, c, col).wait_send())

        when(has_row_below, cross)

    loop(1, arrivals + 1, drain_step)


def per_device(rows, cols, inds, dosages, annotations, window_end):
    depth, tile = dosages.shape
    ann = annotations.shape[0]
    samples = depth * inds
    part = tile // inds
    tiles = 2 * cols - 1
    dma = pltpu.SemaphoreType.DMA
    sems = (dma((2,)), dma((cols,)), dma((cols,)), dma((1,)), dma((1,)), dma((cols,)),
            dma((cols,)), dma((cols,)), dma((cols,)), dma((cols,)), dma((cols,)), dma((cols,)),
            dma((inds - 1, tiles)), dma((inds - 1, tiles)), dma((tiles, 2, inds)),
            dma((2, cols, inds)))
    return pl.pallas_call(
        functools.partial(kernel, rows, cols, inds, samples),
        out_shape=jax.ShapeDtypeStruct((ann, tile), jnp.float32),
        in_specs=[pl.BlockSpec(memory_space=pl.ANY), pl.BlockSpec(memory_space=pl.ANY),
                  pl.BlockSpec(memory_space=pltpu.VMEM)],
        out_specs=pl.BlockSpec(memory_space=pltpu.VMEM),
        scratch_shapes=[
            pltpu.VMEM((cols, depth, tile), jnp.bfloat16),
            pltpu.VMEM((depth, tile), jnp.bfloat16),
            pltpu.VMEM((tile, depth), jnp.bfloat16),
            pltpu.VMEM((tile, depth), jnp.bfloat16),
            pltpu.VMEM((cols, 1, tile), jnp.int32),
            pltpu.VMEM((inds, part, tile), jnp.int32),
            pltpu.VMEM((tiles, inds, part, tile), jnp.float32),
            pltpu.VMEM((inds - 1, tiles, part, tile), jnp.float32),
            pltpu.VMEM((tiles, part, tile), jnp.bfloat16),
            pltpu.VMEM((2, cols, inds, part, tile), jnp.bfloat16),
            pltpu.VMEM((2, cols, ann, tile), jnp.bfloat16),
            sems,
        ],
        compiler_params=pltpu.CompilerParams(collective_id=0, has_side_effects=True),
    )(dosages, annotations, window_end.reshape(1, tile))


def solution(mesh):
    in_specs = (P("ind", ("row", "col")), P("ind", ("row", "col")), P(("row", "col")))
    out_specs = P("ind", ("row", "col"))
    body = functools.partial(per_device, mesh.shape["row"], mesh.shape["col"], mesh.shape["ind"])
    return jax.shard_map(body, mesh=mesh, in_specs=in_specs, out_specs=out_specs, check_vma=False)
```

```python
import functools

import jax
import jax.numpy as jnp
from jax import lax
from jax.experimental import pallas as pl
from jax.experimental.pallas import tpu as pltpu
from jax.sharding import PartitionSpec as P

MESH = pl.DeviceIdType.MESH


def kernel(rows, cols, inds, samples, x_ref, a_ref, w_ref, o_ref, xs, xn, xt, nt, wl, wc,
           gp, rs, sq, sm, am, sems):
    (load_sem, xsend, xrecv, nsend, nrecv, wsend, wrecv, aup, adn, axs, arecv, crecv,
     rsend, rrecv, ssend, srecv) = sems
    r, c, i = lax.axis_index("row"), lax.axis_index("col"), lax.axis_index("ind")
    tile = x_ref.shape[1]
    part = tile // inds
    last = r == rows - 1
    toward = jnp.where(last, -1, 1)
    arrivals = jnp.where(last, c, cols - 1 - c)
    nxt = c - toward
    has_next = (nxt >= 0) & (nxt < cols)
    has_row_below = r < rows - 1
    has_row_above = r > 0

    def dev(row, col, ind):
        return {"row": row, "col": col, "ind": ind}

    def remote(src, dst, send, recv, target):
        return pltpu.make_async_remote_copy(
            src_ref=src, dst_ref=dst, send_sem=send, recv_sem=recv,
            device_id=target, device_id_type=MESH)

    def when(cond, fn):
        pl.when(cond)(fn)

    def loop(lo, hi, fn):
        def body(step, carry):
            fn(step)
            return carry
        lax.fori_loop(lo, hi, body, 0)

    barrier = pltpu.get_barrier_semaphore()

    def greet(row, col, ind):
        pl.semaphore_signal(barrier, inc=1, device_id=dev(row, col, ind), device_id_type=MESH)

    when(c > 0, lambda: greet(r, c - 1, i))
    when(c + 1 < cols, lambda: greet(r, c + 1, i))
    when(has_row_below, lambda: greet(r + 1, c, i))
    when(has_row_above, lambda: greet(r - 1, c, i))
    for k in range(1, inds):
        greet(r, c, lax.rem(i + k, inds))
    near = [c > 0, c + 1 < cols, has_row_below, has_row_above]
    pl.semaphore_wait(barrier, inds - 1 + sum(n.astype(jnp.int32) for n in near))

    def send_x(slot, src):
        return remote(src, xs.at[slot + 1], xsend.at[slot], xrecv.at[slot + 1], dev(r, nxt, i))

    send_up_row = remote(x_ref, xn, nsend.at[0], nrecv.at[0], dev(r - 1, c, i))

    def send_w(slot, src):
        col = c + toward * slot
        return remote(src, wl.at[col], wsend.at[slot], wrecv.at[col], dev(r, nxt, i))

    def a_up(col, src):
        return remote(src, am.at[0, col], aup.at[col], arecv.at[col], dev(r, c + 1, i))

    def a_down(col, src):
        return remote(src, am.at[0, col], adn.at[col], arecv.at[col], dev(r, c - 1, i))

    def a_cross(col, row):
        return remote(am.at[0, col], am.at[1, col], axs.at[col], crecv.at[col], dev(row, c, i))

    when(has_next, lambda: send_x(0, x_ref).start())
    when(has_row_above, lambda: send_up_row.start())
    load_x = pltpu.make_async_copy(x_ref, xs.at[0], load_sem.at[0])
    load_x.start()
    load_a = pltpu.make_async_copy(a_ref, am.at[0, c], load_sem.at[1])
    load_a.start()
    away = cols - 1 - arrivals
    when(has_next, lambda: send_w(0, w_ref).start())
    when(c + 1 < cols, lambda: a_up(c, a_ref).start())
    when(c > 0, lambda: a_down(c, a_ref).start())

    w_own = w_ref[...]
    wl[c] = w_own
    wide = jnp.broadcast_to(w_own.astype(jnp.float32), (tile, tile))
    wc[...] = wide.T.astype(jnp.int32).reshape(inds, part, tile)

    def reduce_send(t, k):
        to = lax.rem(i + k, inds)
        return remote(gp.at[t, to], rs.at[k - 1, t], rsend.at[k - 1, t], rrecv.at[k - 1, t],
                      dev(r, c, to))

    def put_tile(t, value):
        gp[t] = value.reshape(inds, part, tile)
        loop(1, inds, lambda k: reduce_send(t, k).start())

    load_x.wait()
    xt[...] = xs[0].T
    put_tile(0, jnp.dot(xt[...], xs[0], preferred_element_type=jnp.float32))

    def take_next_row():
        send_up_row.wait_recv()
        nt[...] = xn[...].T

    when(has_row_below, take_next_row)

    row_iota = lax.broadcasted_iota(jnp.int32, (part, tile), 0) + i * part
    lane_iota = lax.broadcasted_iota(jnp.int32, (part, tile), 1)

    def s_send(t, which, k, kind, row, col, slot):
        to = lax.rem(i + k, inds)
        return remote(sq.at[t], sm.at[kind, slot, i], ssend.at[t, which, k],
                      srecv.at[kind, slot, i], dev(row, col, to))

    def total_of(t):
        total = gp[t, i]
        for k in range(1, inds):
            reduce_send(t, k).wait_recv()
            total = total + rs[k - 1, t]
        corr = total / samples
        rsq = corr * corr
        return rsq - (1.0 - rsq) / (samples - 2)

    def finish_diag():
        adj = total_of(0)
        base = (r * cols + c) * tile
        ahead = lane_iota >= row_iota
        pos = base + jnp.where(ahead, lane_iota, row_iota)
        lim = jnp.where(ahead, wc[i], jnp.broadcast_to(wl[c], (part, tile)))
        val = jnp.where(pos < lim, adj, 0.0).astype(jnp.bfloat16)
        sq[0] = val
        sm[0, c, i] = val
        loop(1, inds, lambda k: s_send(0, 0, k, 0, r, c, c).start())

    def finish_same(s):
        col = c + toward * s
        adj = total_of(s)
        pos = jnp.where(last, (r * cols + c) * tile + row_iota, (r * cols + col) * tile + lane_iota)
        lim = jnp.where(last, jnp.broadcast_to(wl[col], (part, tile)), wc[i])
        val = jnp.where(pos < lim, adj, 0.0).astype(jnp.bfloat16)
        sq[s] = val
        sm[0, col, i] = val
        loop(0, inds, lambda k: s_send(s, 1, k, 0, r, col, c).start())
        loop(1, inds, lambda k: s_send(s, 0, k, 0, r, c, col).start())

    def finish_cross(s):
        col = c + toward * s
        t = cols - 1 + s
        adj = total_of(t)
        pos = ((r + 1) * cols + c) * tile + row_iota
        lim = jnp.broadcast_to(wl[col], (part, tile))
        sq[t] = jnp.where(pos < lim, adj, 0.0).astype(jnp.bfloat16)
        loop(0, inds, lambda k: s_send(t, 1, k, 1, r, col, c).start())
        loop(0, inds, lambda k: s_send(t, 0, k, 1, r + 1, c, col).start())

    def finish(s):
        finish_same(s)
        when(has_row_below, lambda: finish_cross(s))

    def pass_a(s):
        def from_below():
            col = c - s
            a_up(col, am.at[0, col]).wait_recv()
            when(c + 1 < cols, lambda: a_up(col, am.at[0, col]).start())
            when(has_row_above, lambda: a_cross(col, r - 1).start())

        def from_above():
            col = c + s
            a_down(col, am.at[0, col]).wait_recv()
            when(c > 0, lambda: a_down(col, am.at[0, col]).start())
            when(has_row_below, lambda: a_cross(col, r + 1).start())

        when(c - s >= 0, from_below)
        when(c + s < cols, from_above)

    def step_x(s):
        send_x(s - 1, xs.at[s - 1]).wait_recv()
        when(has_next, lambda: send_x(s, xs.at[s]).start())
        send_w(s, wl.at[c + toward * s]).wait_recv()
        when(has_next, lambda: send_w(s, wl.at[c + toward * s]).start())
        put_tile(s, jnp.dot(xt[...], xs[s], preferred_element_type=jnp.float32))
        when(has_row_below, lambda: put_tile(
            cols - 1 + s, jnp.dot(nt[...], xs[s], preferred_element_type=jnp.float32)))

    def step(s):
        when(s <= arrivals, lambda: step_x(s))
        pass_a(s)
        when(s == 1, finish_diag)
        when((s >= 2) & (s - 1 <= arrivals), lambda: finish(s - 1))

    loop(1, cols, step)
    when(arrivals == cols - 1, lambda: finish(cols - 1))

    load_a.wait()

    def take(kind, slot, q):
        remote(sq.at[0], sm.at[kind, slot, q], ssend.at[0, 0, 0], srecv.at[kind, slot, q],
               dev(r, c, lax.rem(i + 1, inds))).wait_recv()

    def add(kind, slot, flip):
        lhs = am[kind, slot]
        rhs = sm[kind, slot].reshape(tile, tile)
        dims = (((1,), (1,)), ((), ())) if flip else (((1,), (0,)), ((), ()))
        o_ref[...] += lax.dot_general(lhs, rhs, dims, preferred_element_type=jnp.float32)

    loop(1, inds, lambda k: take(0, c, lax.rem(i + k, inds)))
    o_ref[...] = lax.dot_general(am[0, c], sm[0, c].reshape(tile, tile),
                                 (((1,), (0,)), ((), ())), preferred_element_type=jnp.float32)

    def add_home(s):
        col = c + toward * s
        loop(1, inds, lambda k: take(0, col, lax.rem(i + k, inds)))
        add(0, col, True)

    loop(1, arrivals + 1, add_home)

    def add_away(s):
        col = c - toward * s
        loop(0, inds, lambda q: take(0, col, q))
        add(0, col, False)

    loop(1, away + 1, add_away)

    def add_cross(col):
        a_cross_wait = remote(am.at[0, col], am.at[1, col], axs.at[col], crecv.at[col],
                              dev(r, nxt, i))
        a_cross_wait.wait_recv()
        loop(0, inds, lambda q: take(1, col, q))
        when(col < c, lambda: add(1, col, False))
        when(col > c, lambda: add(1, col, True))

    when(has_row_below, lambda: loop(0, c, add_cross))
    when(has_row_above, lambda: loop(c + 1, cols, add_cross))

    when(has_next, lambda: loop(0, arrivals + 1, lambda s: send_x(s, xs.at[s]).wait_send()))
    when(has_row_above, lambda: send_up_row.wait_send())
    when(has_next, lambda: loop(0, arrivals + 1, lambda s: send_w(s, wl.at[c + toward * s]).wait_send()))
    when(c + 1 < cols, lambda: loop(0, c + 1, lambda q: a_up(q, am.at[0, q]).wait_send()))
    when(c > 0, lambda: loop(c, cols, lambda q: a_down(q, am.at[0, q]).wait_send()))
    when(has_row_above, lambda: loop(0, c, lambda q: a_cross(q, r - 1).wait_send()))
    when(has_row_below, lambda: loop(c + 1, cols, lambda q: a_cross(q, r + 1).wait_send()))

    def drain(t, kind, row, col):
        loop(1, inds, lambda k: reduce_send(t, k).wait_send())
        loop(0, inds, lambda k: s_send(t, 1, k, kind, r, col, c).wait_send())

    loop(1, inds, lambda k: reduce_send(0, k).wait_send())
    loop(1, inds, lambda k: s_send(0, 0, k, 0, r, c, c).wait_send())

    def drain_step(s):
        col = c + toward * s
        drain(s, 0, r, col)
        loop(1, inds, lambda k: s_send(s, 0, k, 0, r, c, col).wait_send())

        def cross():
            drain(cols - 1 + s, 1, r, col)
            loop(0, inds, lambda k: s_send(cols - 1 + s, 0, k, 1, r + 1, c, col).wait_send())

        when(has_row_below, cross)

    loop(1, arrivals + 1, drain_step)


def per_device(rows, cols, inds, dosages, annotations, window_end):
    depth, tile = dosages.shape
    ann = annotations.shape[0]
    samples = depth * inds
    part = tile // inds
    tiles = 2 * cols - 1
    dma = pltpu.SemaphoreType.DMA
    sems = (dma((2,)), dma((cols,)), dma((cols,)), dma((1,)), dma((1,)), dma((cols,)),
            dma((cols,)), dma((cols,)), dma((cols,)), dma((cols,)), dma((cols,)), dma((cols,)),
            dma((inds - 1, tiles)), dma((inds - 1, tiles)), dma((tiles, 2, inds)),
            dma((2, cols, inds)))
    return pl.pallas_call(
        functools.partial(kernel, rows, cols, inds, samples),
        out_shape=jax.ShapeDtypeStruct((ann, tile), jnp.float32),
        in_specs=[pl.BlockSpec(memory_space=pl.ANY), pl.BlockSpec(memory_space=pl.ANY),
                  pl.BlockSpec(memory_space=pltpu.VMEM)],
        out_specs=pl.BlockSpec(memory_space=pltpu.VMEM),
        scratch_shapes=[
            pltpu.VMEM((cols, depth, tile), jnp.bfloat16),
            pltpu.VMEM((depth, tile), jnp.bfloat16),
            pltpu.VMEM((tile, depth), jnp.bfloat16),
            pltpu.VMEM((tile, depth), jnp.bfloat16),
            pltpu.VMEM((cols, 1, tile), jnp.int32),
            pltpu.VMEM((inds, part, tile), jnp.int32),
            pltpu.VMEM((tiles, inds, part, tile), jnp.float32),
            pltpu.VMEM((inds - 1, tiles, part, tile), jnp.float32),
            pltpu.VMEM((tiles, part, tile), jnp.bfloat16),
            pltpu.VMEM((2, cols, inds, part, tile), jnp.bfloat16),
            pltpu.VMEM((2, cols, ann, tile), jnp.bfloat16),
            sems,
        ],
        compiler_params=pltpu.CompilerParams(collective_id=0, has_side_effects=True),
    )(dosages, annotations, window_end.reshape(1, tile))


def solution(mesh):
    in_specs = (P("ind", ("row", "col")), P("ind", ("row", "col")), P(("row", "col")))
    out_specs = P("ind", ("row", "col"))
    body = functools.partial(per_device, mesh.shape["row"], mesh.shape["col"], mesh.shape["ind"])
    return jax.shard_map(body, mesh=mesh, in_specs=in_specs, out_specs=out_specs, check_vma=False)
```

```python
import functools

import jax
import jax.numpy as jnp
from jax import lax
from jax.experimental import pallas as pl
from jax.experimental.pallas import tpu as pltpu
from jax.sharding import PartitionSpec as P

MESH = pl.DeviceIdType.MESH


def kernel(rows, cols, inds, samples, x_ref, a_ref, w_ref, o_ref, xs, xn, xt, wl, wc,
           gp, rs, sq, sm, am, sems):
    (load_sem, xsend, xrecv, nsend, nrecv, wsend, wrecv, aup, adn, axs, arecv, crecv,
     rrecv, ssend, srecv) = sems
    r, c, i = lax.axis_index("row"), lax.axis_index("col"), lax.axis_index("ind")
    tile = x_ref.shape[1]
    part = tile // inds
    right_hub = cols // 2
    left_hub = right_hub - 1
    span = max(right_hub, cols - right_hub)
    last = r == rows - 1
    has_row_below = r < rows - 1
    has_row_above = r > 0
    main = jnp.where(last, right_hub, left_hub)
    is_main = c == main
    is_hub = (c == left_hub) | (c == right_hub)
    on_left = c <= left_hub
    low = jnp.where(on_left, 0, right_hub)
    high = jnp.where(on_left, left_hub, cols - 1)
    nxt = jnp.where(c < main, c + 1, c - 1)
    takes_left = c <= main
    takes_right = c >= main

    def dev(row, col, ind):
        return {"row": row, "col": col, "ind": ind}

    def remote(src, dst, send, recv, target):
        return pltpu.make_async_remote_copy(
            src_ref=src, dst_ref=dst, send_sem=send, recv_sem=recv,
            device_id=target, device_id_type=MESH)

    def when(cond, fn):
        pl.when(cond)(fn)

    def loop(lo, hi, fn):
        def body(step, carry):
            fn(step)
            return carry
        lax.fori_loop(lo, hi, body, 0)

    barrier = pltpu.get_barrier_semaphore()

    def greet(row, col, ind):
        pl.semaphore_signal(barrier, inc=1, device_id=dev(row, col, ind), device_id_type=MESH)

    when(c > 0, lambda: greet(r, c - 1, i))
    when(c + 1 < cols, lambda: greet(r, c + 1, i))
    when(has_row_below, lambda: greet(r + 1, c, i))
    when(has_row_above, lambda: greet(r - 1, c, i))
    for k in range(1, inds):
        greet(r, c, lax.rem(i + k, inds))
    load_x = pltpu.make_async_copy(x_ref, xs.at[c], load_sem.at[0])
    load_x.start()
    load_a = pltpu.make_async_copy(a_ref, am.at[0, c], load_sem.at[1])
    load_a.start()
    near = [c > 0, c + 1 < cols, has_row_below, has_row_above]
    pl.semaphore_wait(barrier, inds - 1 + sum(n.astype(jnp.int32) for n in near))

    def send_x(col, src):
        return remote(src, xs.at[col], xsend.at[col], xrecv.at[col], dev(r, nxt, i))

    def send_w(col, src):
        return remote(src, wl.at[col], wsend.at[col], wrecv.at[col], dev(r, nxt, i))

    def send_n(col, src):
        slot = col - low
        return remote(src, xn.at[slot], nsend.at[slot], nrecv.at[slot], dev(r - 1, c, i))

    def a_up(col, src):
        return remote(src, am.at[0, col], aup.at[col], arecv.at[col], dev(r, c + 1, i))

    def a_down(col, src):
        return remote(src, am.at[0, col], adn.at[col], arecv.at[col], dev(r, c - 1, i))

    def a_cross(col, row):
        return remote(am.at[0, col], am.at[1, col], axs.at[col], crecv.at[col], dev(row, c, i))

    def gives_n(col):
        return has_row_above & is_hub & (col >= low) & (col <= high) & (col < cols - 1)

    when(~is_main, lambda: send_x(c, x_ref).start())
    when(~is_main, lambda: send_w(c, w_ref).start())
    when(gives_n(c), lambda: send_n(c, x_ref).start())
    when(c + 1 < cols, lambda: a_up(c, a_ref).start())
    when(c > 0, lambda: a_down(c, a_ref).start())
    wl[c] = w_ref[...]

    def valid(kind, p, q):
        if kind:
            return has_row_below & (p < q) & ((q >= low) | is_main)
        return jnp.where(last, p >= q, p <= q) & (is_main | ((q >= low) & (q <= high)))

    def away(col):
        return jnp.abs(col - c)

    def ready(kind, p, q):
        return jnp.maximum(away(p) + kind, away(q))

    def reduce_send(kind, l, q, k):
        to = lax.rem(i + k, inds)
        return remote(gp.at[kind, l, q, to], rs.at[k - 1, kind, l, q], ssend.at[kind, l, q, 0, k],
                      rrecv.at[k - 1, kind, l, q], dev(r, c, to))

    def put_tile(kind, l, q):
        value = jnp.dot(xt[kind, l], xs[q], preferred_element_type=jnp.float32)
        gp[kind, l, q] = value.reshape(inds, part, tile)
        loop(1, inds, lambda k: reduce_send(kind, l, q, k).start())

    def use(col, before):
        def turn():
            l = col - low
            xt[0, l] = xs[col].T
            wide = jnp.broadcast_to(wl[col].astype(jnp.float32), (tile, tile))
            wc[l] = wide.T.astype(jnp.int32).reshape(inds, part, tile)

        mine = (col >= low) & (col <= high)
        when(mine, turn)

        def as_q(l):
            p = low + l
            when(((p == col) | before(p)) & (p <= high) & valid(0, p, col),
                 lambda: put_tile(0, l, col))
            when((away(p) + 1 <= away(col)) & (p <= high) & valid(1, p, col),
                 lambda: put_tile(1, l, col))

        loop(0, span, as_q)
        when(mine, lambda: loop(0, cols, lambda q: when(
            before(q) & valid(0, col, q), lambda: put_tile(0, col - low, q))))

    def use_next(col, step):
        l = col - low
        send_n(col, x_ref).wait_recv()
        xt[1, l] = xn[l].T
        loop(0, cols, lambda q: when(
            (away(q) < step) & valid(1, col, q), lambda: put_tile(1, l, q)))

    row_iota = lax.broadcasted_iota(jnp.int32, (part, tile), 0) + i * part
    lane_iota = lax.broadcasted_iota(jnp.int32, (part, tile), 1)

    def s_send(kind, l, q, which, k, row, col, slot):
        to = lax.rem(i + k, inds)
        return remote(sq.at[kind, l, q], sm.at[kind, slot, i], ssend.at[kind, l, q, which, k],
                      srecv.at[kind, slot, i], dev(row, col, to))

    def targets(kind, l, q, act, keep):
        p = low + l
        here = q == c

        def second():
            when(here, keep(q, p))
            first = here.astype(jnp.int32)
            loop(first, inds, lambda k: act(s_send(kind, l, q, 1, k, r, q, p)))

        def same_row():
            when(p == c, keep(p, q))
            first = (p == c).astype(jnp.int32)
            loop(first, inds, lambda k: act(s_send(kind, l, q, 0, k, r, p, q)))

        if kind:
            second()
            loop(0, inds, lambda k: act(s_send(kind, l, q, 0, k, r + 1, p, q)))
        else:
            when(p != q, second)
            same_row()

    def finish(kind, l, q):
        p = low + l
        total = gp[kind, l, q, i]
        for k in range(1, inds):
            reduce_send(kind, l, q, k).wait()
            total = total + rs[k - 1, kind, l, q]
        corr = total / samples
        rsq = corr * corr
        adj = rsq - (1.0 - rsq) / (samples - 2)
        by_lane = jnp.broadcast_to(wl[q], (part, tile))
        if kind:
            pos, lim = ((r + 1) * cols + p) * tile + row_iota, by_lane
        else:
            rows_first = ((p == q) & (lane_iota >= row_iota)) | ((p != q) & ~last)
            pos = jnp.where(rows_first, (r * cols + q) * tile + lane_iota,
                            (r * cols + p) * tile + row_iota)
            lim = jnp.where(rows_first, wc[l, i], by_lane)
        val = jnp.where(pos < lim, adj, 0.0).astype(jnp.bfloat16)
        sq[kind, l, q] = val

        def keep(me, slot):
            def store():
                sm[kind, slot, i] = val
            return store

        targets(kind, l, q, lambda copy: copy.start(), keep)

    def each_tile(fn):
        for kind in range(2):
            def by_l(l, kind=kind):
                def by_q(q):
                    p = low + l
                    when((p <= high) & valid(kind, p, q), lambda: fn(kind, l, q, ready(kind, p, q)))
                loop(0, cols, by_q)
            loop(0, span, by_l)

    def pass_a(s):
        def from_left():
            col = c - s
            a_up(col, am.at[0, col]).wait_recv()
            when(c + 1 < cols, lambda: a_up(col, am.at[0, col]).start())
            when(has_row_above, lambda: a_cross(col, r - 1).start())

        def from_right():
            col = c + s
            a_down(col, am.at[0, col]).wait_recv()
            when(c > 0, lambda: a_down(col, am.at[0, col]).start())
            when(has_row_below, lambda: a_cross(col, r + 1).start())

        when(c - s >= 0, from_left)
        when(c + s < cols, from_right)

    def arrive(col, before):
        send_x(col, xs.at[col]).wait_recv()
        when(~is_main, lambda: send_x(col, xs.at[col]).start())
        when(gives_n(col), lambda: send_n(col, xs.at[col]).start())
        send_w(col, wl.at[col]).wait_recv()
        when(~is_main, lambda: send_w(col, wl.at[col]).start())
        when(is_hub, lambda: use(col, before))

    def needs_n(col):
        return has_row_below & is_hub & (col >= low) & (col <= high) & (col < cols - 1)

    load_x.wait()
    when(is_hub, lambda: use(c, lambda x: x < 0))

    def step(s):
        left, right = c - s + 1, c + s - 1
        when((left >= 0) & needs_n(left), lambda: use_next(left, s))
        when((s > 1) & (right < cols) & needs_n(right), lambda: use_next(right, s))
        left, right = c - s, c + s
        when((left >= 0) & takes_left, lambda: arrive(left, lambda x: away(x) < s))
        when((right < cols) & takes_right, lambda: arrive(
            right, lambda x: (away(x) < s) | (x == c - s)))
        when(is_hub, lambda: each_tile(lambda kind, l, q, t: when(
            t == s - 1, lambda: finish(kind, l, q))))
        when(s < cols, lambda: pass_a(s))

    steps = span + 2
    loop(1, steps, step)
    when(is_hub, lambda: each_tile(lambda kind, l, q, t: when(
        t >= steps - 1, lambda: finish(kind, l, q))))
    loop(steps, cols, pass_a)

    load_a.wait()

    def take(kind, slot, q):
        remote(sq.at[0, 0, 0], sm.at[kind, slot, q], ssend.at[0, 0, 0, 0, 0],
               srecv.at[kind, slot, q], dev(r, c, lax.rem(i + 1, inds))).wait_recv()

    def take_all(kind, slot, p, same_row):
        home = jnp.where(p <= left_hub, left_hub, right_hub)
        first = (same_row & (home == c)).astype(jnp.int32)
        loop(first, inds, lambda k: take(kind, slot, lax.rem(i + k, inds)))

    def add(kind, slot, flip):
        lhs = am[kind, slot]
        rhs = sm[kind, slot].reshape(tile, tile)
        dims = (((1,), (1,)), ((), ())) if flip else (((1,), (0,)), ((), ()))
        o_ref[...] += lax.dot_general(lhs, rhs, dims, preferred_element_type=jnp.float32)

    o_ref[...] = jnp.zeros_like(o_ref)

    def add_row(col):
        p = jnp.where(last, jnp.maximum(c, col), jnp.minimum(c, col))
        take_all(0, col, p, c >= 0)
        when(p == c, lambda: add(0, col, True))
        when(p != c, lambda: add(0, col, False))

    loop(0, cols, add_row)

    def add_cross(col):
        remote(am.at[0, col], am.at[1, col], axs.at[col], crecv.at[col],
               dev(r, nxt, i)).wait_recv()
        take_all(1, col, jnp.minimum(c, col), col < c)
        when(col < c, lambda: add(1, col, False))
        when(col > c, lambda: add(1, col, True))

    when(has_row_below, lambda: loop(0, c, add_cross))
    when(has_row_above, lambda: loop(c + 1, cols, add_cross))

    def sent_x(col):
        send_x(col, xs.at[col]).wait_send()
        send_w(col, wl.at[col]).wait_send()

    when(c < main, lambda: loop(0, c + 1, sent_x))
    when(c > main, lambda: loop(c, cols, sent_x))
    loop(low, high + 1, lambda col: when(
        gives_n(col), lambda: send_n(col, xs.at[col]).wait_send()))
    when(c + 1 < cols, lambda: loop(0, c + 1, lambda q: a_up(q, am.at[0, q]).wait_send()))
    when(c > 0, lambda: loop(c, cols, lambda q: a_down(q, am.at[0, q]).wait_send()))
    when(has_row_above, lambda: loop(0, c, lambda q: a_cross(q, r - 1).wait_send()))
    when(has_row_below, lambda: loop(c + 1, cols, lambda q: a_cross(q, r + 1).wait_send()))

    def drain(kind, l, q, t):
        targets(kind, l, q, lambda copy: copy.wait_send(), lambda me, slot: lambda: None)

    when(is_hub, lambda: each_tile(drain))


def per_device(rows, cols, inds, dosages, annotations, window_end):
    depth, tile = dosages.shape
    ann = annotations.shape[0]
    samples = depth * inds
    part = tile // inds
    span = max(cols // 2, cols - cols // 2)
    dma = pltpu.SemaphoreType.DMA
    sems = (dma((2,)), dma((cols,)), dma((cols,)), dma((span,)), dma((span,)), dma((cols,)),
            dma((cols,)), dma((cols,)), dma((cols,)), dma((cols,)), dma((cols,)), dma((cols,)),
            dma((inds - 1, 2, span, cols)),
            dma((2, span, cols, 2, inds)), dma((2, cols, inds)))
    return pl.pallas_call(
        functools.partial(kernel, rows, cols, inds, samples),
        out_shape=jax.ShapeDtypeStruct((ann, tile), jnp.float32),
        in_specs=[pl.BlockSpec(memory_space=pl.ANY), pl.BlockSpec(memory_space=pl.ANY),
                  pl.BlockSpec(memory_space=pltpu.VMEM)],
        out_specs=pl.BlockSpec(memory_space=pltpu.VMEM),
        scratch_shapes=[
            pltpu.VMEM((cols, depth, tile), jnp.bfloat16),
            pltpu.VMEM((span, depth, tile), jnp.bfloat16),
            pltpu.VMEM((2, span, tile, depth), jnp.bfloat16),
            pltpu.VMEM((cols, 1, tile), jnp.int32),
            pltpu.VMEM((span, inds, part, tile), jnp.int32),
            pltpu.VMEM((2, span, cols, inds, part, tile), jnp.float32),
            pltpu.VMEM((inds - 1, 2, span, cols, part, tile), jnp.float32),
            pltpu.VMEM((2, span, cols, part, tile), jnp.bfloat16),
            pltpu.VMEM((2, cols, inds, part, tile), jnp.bfloat16),
            pltpu.VMEM((2, cols, ann, tile), jnp.bfloat16),
            sems,
        ],
        compiler_params=pltpu.CompilerParams(collective_id=0, has_side_effects=True),
    )(dosages, annotations, window_end.reshape(1, tile))


def solution(mesh):
    in_specs = (P("ind", ("row", "col")), P("ind", ("row", "col")), P(("row", "col")))
    out_specs = P("ind", ("row", "col"))
    body = functools.partial(per_device, mesh.shape["row"], mesh.shape["col"], mesh.shape["ind"])
    return jax.shard_map(body, mesh=mesh, in_specs=in_specs, out_specs=out_specs, check_vma=False)
```

```python
import functools

import jax
import jax.numpy as jnp
from jax import lax
from jax.experimental import pallas as pl
from jax.experimental.pallas import tpu as pltpu
from jax.sharding import PartitionSpec as P

MESH = pl.DeviceIdType.MESH


def kernel(rows, cols, inds, samples, x_ref, a_ref, w_ref, o_ref, xs, xn, xt, wl, wc,
           gp, rs, sq, smq, smp, am, sems):
    (load_sem, xsend, xrecv, nsend, nrecv, wsend, wrecv, aup, adn, axs, arecv, crecv,
     rsend, rrecv, qsend, qrecv, psend, precv) = sems
    r, c, i = lax.axis_index("row"), lax.axis_index("col"), lax.axis_index("ind")
    tile = x_ref.shape[1]
    part = tile // inds
    right_hub = cols // 2
    left_hub = right_hub - 1
    span = max(right_hub, cols - right_hub)
    last = r == rows - 1
    has_row_below = r < rows - 1
    has_row_above = r > 0
    main = jnp.where(last, right_hub, left_hub)
    is_main = c == main
    is_hub = (c == left_hub) | (c == right_hub)
    on_left = c <= left_hub
    low = jnp.where(on_left, 0, right_hub)
    high = jnp.where(on_left, left_hub, cols - 1)
    nxt = jnp.where(c < main, c + 1, c - 1)
    takes_left = c <= main
    takes_right = c >= main

    def dev(row, col, ind):
        return {"row": row, "col": col, "ind": ind}

    def remote(src, dst, send, recv, target):
        return pltpu.make_async_remote_copy(
            src_ref=src, dst_ref=dst, send_sem=send, recv_sem=recv,
            device_id=target, device_id_type=MESH)

    def when(cond, fn):
        pl.when(cond)(fn)

    def loop(lo, hi, fn):
        def body(step, carry):
            fn(step)
            return carry
        lax.fori_loop(lo, hi, body, 0)

    barrier = pltpu.get_barrier_semaphore()

    def greet(row, col, ind):
        pl.semaphore_signal(barrier, inc=1, device_id=dev(row, col, ind), device_id_type=MESH)

    when(c > 0, lambda: greet(r, c - 1, i))
    when(c + 1 < cols, lambda: greet(r, c + 1, i))
    when(has_row_below, lambda: greet(r + 1, c, i))
    when(has_row_above, lambda: greet(r - 1, c, i))
    for k in range(1, inds):
        greet(r, c, lax.rem(i + k, inds))
    load_x = pltpu.make_async_copy(x_ref, xs.at[c], load_sem.at[0])
    load_x.start()
    load_a = pltpu.make_async_copy(a_ref, am.at[0, c], load_sem.at[1])
    load_a.start()
    near = [c > 0, c + 1 < cols, has_row_below, has_row_above]
    pl.semaphore_wait(barrier, inds - 1 + sum(n.astype(jnp.int32) for n in near))

    def send_x(col, src):
        return remote(src, xs.at[col], xsend.at[col], xrecv.at[col], dev(r, nxt, i))

    def send_w(col, src):
        return remote(src, wl.at[col], wsend.at[col], wrecv.at[col], dev(r, nxt, i))

    def send_n(col, src):
        slot = col - low
        return remote(src, xn.at[slot], nsend.at[slot], nrecv.at[slot], dev(r - 1, c, i))

    def a_up(col, src):
        return remote(src, am.at[0, col], aup.at[col], arecv.at[col], dev(r, c + 1, i))

    def a_down(col, src):
        return remote(src, am.at[0, col], adn.at[col], arecv.at[col], dev(r, c - 1, i))

    def a_cross(col, row):
        return remote(am.at[0, col], am.at[1, col], axs.at[col], crecv.at[col], dev(row, c, i))

    def gives_n(col):
        return has_row_above & is_hub & (col >= low) & (col <= high) & (col < cols - 1)

    when(~is_main, lambda: send_x(c, x_ref).start())
    when(~is_main, lambda: send_w(c, w_ref).start())
    when(gives_n(c), lambda: send_n(c, x_ref).start())
    when(c + 1 < cols, lambda: a_up(c, a_ref).start())
    when(c > 0, lambda: a_down(c, a_ref).start())
    wl[c] = w_ref[...]

    def valid(kind, p, q):
        if kind:
            return has_row_below & (p < q)
        return jnp.where(last, p >= q, p <= q)

    def has_q(q):
        return is_main | ((q >= low) & (q <= high))

    def away(col):
        return jnp.abs(col - c)

    def reduce_send(q, k):
        to = lax.rem(i + k, inds)
        return remote(gp.at[q, to], rs.at[k - 1, q], rsend.at[k - 1, q], rrecv.at[k - 1, q],
                      dev(r, c, to))

    def multiply(q):
        depth = xs.shape[1]
        value = jnp.dot(xt[...].reshape(2 * span * tile, depth), xs[q],
                        preferred_element_type=jnp.float32)
        value = value.reshape(2, span, inds, part, tile)
        for to in range(inds):
            gp[q, to] = value[:, :, to]
        for k in range(1, inds):
            reduce_send(q, k).start()

    def turn(col):
        l = col - low
        xt[0, l] = xs[col].T
        wide = jnp.broadcast_to(wl[col].astype(jnp.float32), (tile, tile))
        wc[l] = wide.T.astype(jnp.int32).reshape(inds, part, tile)

    def turn_next(col):
        l = col - low
        send_n(col, x_ref).wait_recv()
        xt[1, l] = xn[l].T

    row_iota = lax.broadcasted_iota(jnp.int32, (part, tile), 0) + i * part
    lane_iota = lax.broadcasted_iota(jnp.int32, (part, tile), 1)
    side = jnp.where(on_left, 0, 1)

    def to_q(q, k):
        return remote(sq.at[q], smq.at[i, :, pl.ds(low, span)], qsend.at[q, k],
                      qrecv.at[i, side], dev(r, q, lax.rem(i + k, inds)))

    def to_p(kind, l, q, k):
        return remote(sq.at[q, kind, l], smp.at[i, kind, q], psend.at[q, kind, l, k],
                      precv.at[i, kind, q], dev(r + kind, low + l, lax.rem(i + k, inds)))

    def sends(q, act):
        loop((q == c).astype(jnp.int32), inds, lambda k: act(to_q(q, k)))
        for kind in range(2):
            for l in range(span):
                p = low + l
                first = 0 if kind else (p == c).astype(jnp.int32)

                def go(kind=kind, l=l, first=first):
                    loop(first, inds, lambda k: act(to_p(kind, l, q, k)))

                when((p != q) & valid(kind, p, q), go)

    def finish(q):
        total = gp[q, i]
        for k in range(1, inds):
            reduce_send(q, k).wait_recv()
            total = total + rs[k - 1, q]
        corr = total / samples
        rsq = corr * corr
        adj = rsq - (1.0 - rsq) / (samples - 2)
        by_lane = jnp.broadcast_to(wl[q], (part, tile))
        for kind in range(2):
            for l in range(span):
                p = low + l
                if kind:
                    pos, lim = ((r + 1) * cols + p) * tile + row_iota, by_lane
                else:
                    rows_first = ((p == q) & (lane_iota >= row_iota)) | ((p != q) & ~last)
                    pos = jnp.where(rows_first, (r * cols + q) * tile + lane_iota,
                                    (r * cols + p) * tile + row_iota)
                    lim = jnp.where(rows_first, wc[l, i], by_lane)
                val = jnp.where(pos < lim, adj[kind, l], 0.0).astype(jnp.bfloat16)
                sq[q, kind, l] = val
        sends(q, lambda copy: copy.start())

        def keep_q():
            smq[i, :, pl.ds(low, span)] = sq[q]

        when(q == c, keep_q)

        def keep_p():
            smp[i, 0, q] = sq[q, 0, c - low]

        when(q != c, keep_p)

    def pass_a(s):
        def from_left():
            col = c - s
            a_up(col, am.at[0, col]).wait_recv()
            when(c + 1 < cols, lambda: a_up(col, am.at[0, col]).start())
            when(has_row_above, lambda: a_cross(col, r - 1).start())

        def from_right():
            col = c + s
            a_down(col, am.at[0, col]).wait_recv()
            when(c > 0, lambda: a_down(col, am.at[0, col]).start())
            when(has_row_below, lambda: a_cross(col, r + 1).start())

        when(c - s >= 0, from_left)
        when(c + s < cols, from_right)

    def in_l(col):
        return is_hub & (col >= low) & (col <= high)

    def arrive(col):
        send_x(col, xs.at[col]).wait_recv()
        when(~is_main, lambda: send_x(col, xs.at[col]).start())
        when(gives_n(col), lambda: send_n(col, xs.at[col]).start())
        send_w(col, wl.at[col]).wait_recv()
        when(~is_main, lambda: send_w(col, wl.at[col]).start())
        when(in_l(col), lambda: turn(col))

    def arrivals(s):
        left, right = c - s, c + s
        when((left >= 0) & takes_left, lambda: arrive(left))
        when((right < cols) & takes_right, lambda: arrive(right))

    def each_q(cond, fn):
        when(is_hub, lambda: loop(0, cols, lambda q: when(
            has_q(q) & cond(away(q)), lambda: fn(q))))

    load_x.wait()
    when(is_hub, lambda: turn(c))

    def step(s):
        arrivals(s)
        pass_a(s)

    loop(1, span, step)
    loop(low, high + 1, lambda col: when(
        in_l(col) & has_row_below & (col < cols - 1), lambda: turn_next(col)))
    each_q(lambda d: d < span, multiply)
    arrivals(span)
    each_q(lambda d: d >= span, multiply)
    loop(span, cols, pass_a)
    each_q(lambda d: d < span, finish)
    each_q(lambda d: d >= span, finish)

    load_a.wait()

    def take_q(which):
        home = jnp.where(which == 0, left_hub, right_hub)
        first = (home == c).astype(jnp.int32)
        loop(first, inds, lambda k: remote(
            sq.at[0], smq.at[lax.rem(i + k, inds), :, pl.ds(which * right_hub, span)],
            qsend.at[0, 0], qrecv.at[lax.rem(i + k, inds), which], dev(r, c, i)).wait_recv())

    def take_p(kind, q, first):
        loop(first, inds, lambda k: remote(
            sq.at[0, 0, 0], smp.at[lax.rem(i + k, inds), kind, q], psend.at[0, 0, 0, 0],
            precv.at[lax.rem(i + k, inds), kind, q], dev(r, c, i)).wait_recv())

    def add(lhs, rhs, axis):
        o_ref[...] += lax.dot_general(lhs, rhs.reshape(tile, tile), (((1,), (axis,)), ((), ())),
                                      preferred_element_type=jnp.float32)

    o_ref[...] = jnp.zeros_like(o_ref)
    hub_first = is_hub.astype(jnp.int32)

    def as_p(q):
        take_p(0, q, hub_first)
        add(am[0, q], smp[:, 0, q], 1)

    loop(jnp.where(last, 0, c + 1), jnp.where(last, c, cols), as_p)

    def wait_cross(col):
        remote(am.at[0, col], am.at[1, col], axs.at[col], crecv.at[col],
               dev(r, nxt, i)).wait_recv()

    def as_next_p(q):
        wait_cross(q)
        take_p(1, q, 0)
        add(am[1, q], smp[:, 1, q], 1)

    when(has_row_above, lambda: loop(c + 1, cols, as_next_p))
    when(~last, lambda: take_q(0))
    when(~last & ~on_left, lambda: take_q(1))
    when(last, lambda: take_q(1))
    when(last & on_left, lambda: take_q(0))
    loop(jnp.where(last, c, 0), jnp.where(last, cols, c + 1),
         lambda p: add(am[0, p], smq[:, 0, p], 0))

    def as_q_cross(p):
        wait_cross(p)
        add(am[1, p], smq[:, 1, p], 0)

    when(has_row_below, lambda: loop(0, c, as_q_cross))

    def sent_x(col):
        send_x(col, xs.at[col]).wait_send()
        send_w(col, wl.at[col]).wait_send()

    when(c < main, lambda: loop(0, c + 1, sent_x))
    when(c > main, lambda: loop(c, cols, sent_x))
    loop(low, high + 1, lambda col: when(
        gives_n(col), lambda: send_n(col, xs.at[col]).wait_send()))
    when(c + 1 < cols, lambda: loop(0, c + 1, lambda q: a_up(q, am.at[0, q]).wait_send()))
    when(c > 0, lambda: loop(c, cols, lambda q: a_down(q, am.at[0, q]).wait_send()))
    when(has_row_above, lambda: loop(0, c, lambda q: a_cross(q, r - 1).wait_send()))
    when(has_row_below, lambda: loop(c + 1, cols, lambda q: a_cross(q, r + 1).wait_send()))

    def drain(q):
        for k in range(1, inds):
            reduce_send(q, k).wait_send()
        sends(q, lambda copy: copy.wait_send())

    each_q(lambda d: d >= 0, drain)


def per_device(rows, cols, inds, dosages, annotations, window_end):
    depth, tile = dosages.shape
    ann = annotations.shape[0]
    samples = depth * inds
    part = tile // inds
    span = max(cols // 2, cols - cols // 2)
    dma = pltpu.SemaphoreType.DMA
    sems = (dma((2,)), dma((cols,)), dma((cols,)), dma((span,)), dma((span,)), dma((cols,)),
            dma((cols,)), dma((cols,)), dma((cols,)), dma((cols,)), dma((cols,)), dma((cols,)),
            dma((inds - 1, cols)), dma((inds - 1, cols)), dma((cols, inds)), dma((inds, 2)),
            dma((cols, 2, span, inds)), dma((inds, 2, cols)))
    return pl.pallas_call(
        functools.partial(kernel, rows, cols, inds, samples),
        out_shape=jax.ShapeDtypeStruct((ann, tile), jnp.float32),
        in_specs=[pl.BlockSpec(memory_space=pl.ANY), pl.BlockSpec(memory_space=pl.ANY),
                  pl.BlockSpec(memory_space=pltpu.VMEM)],
        out_specs=pl.BlockSpec(memory_space=pltpu.VMEM),
        scratch_shapes=[
            pltpu.VMEM((cols, depth, tile), jnp.bfloat16),
            pltpu.VMEM((span, depth, tile), jnp.bfloat16),
            pltpu.VMEM((2, span, tile, depth), jnp.bfloat16),
            pltpu.VMEM((cols, 1, tile), jnp.int32),
            pltpu.VMEM((span, inds, part, tile), jnp.int32),
            pltpu.VMEM((cols, inds, 2, span, part, tile), jnp.float32),
            pltpu.VMEM((inds - 1, cols, 2, span, part, tile), jnp.float32),
            pltpu.VMEM((cols, 2, span, part, tile), jnp.bfloat16),
            pltpu.VMEM((inds, 2, cols, part, tile), jnp.bfloat16),
            pltpu.VMEM((inds, 2, cols, part, tile), jnp.bfloat16),
            pltpu.VMEM((2, cols, ann, tile), jnp.bfloat16),
            sems,
        ],
        compiler_params=pltpu.CompilerParams(collective_id=0, has_side_effects=True),
    )(dosages, annotations, window_end.reshape(1, tile))


def solution(mesh):
    in_specs = (P("ind", ("row", "col")), P("ind", ("row", "col")), P(("row", "col")))
    out_specs = P("ind", ("row", "col"))
    body = functools.partial(per_device, mesh.shape["row"], mesh.shape["col"], mesh.shape["ind"])
    return jax.shard_map(body, mesh=mesh, in_specs=in_specs, out_specs=out_specs, check_vma=False)
```

```python
import functools

import jax
import jax.numpy as jnp
from jax import lax
from jax.experimental import pallas as pl
from jax.experimental.pallas import tpu as pltpu
from jax.sharding import PartitionSpec as P

MESH = pl.DeviceIdType.MESH


def kernel(rows, cols, inds, samples, x_ref, a_ref, w_ref, o_ref, xs, xn, xt, wl, wc,
           gp, rs, sq, sm, am, sems):
    (load_sem, xsend, xrecv, nsend, nrecv, wsend, wrecv, aup, adn, axs, arecv, crecv,
     rrecv, ssend, srecv) = sems
    r, c, i = lax.axis_index("row"), lax.axis_index("col"), lax.axis_index("ind")
    tile = x_ref.shape[1]
    part = tile // inds
    right_hub = cols // 2
    left_hub = right_hub - 1
    span = max(right_hub, cols - right_hub)
    last = r == rows - 1
    has_row_below = r < rows - 1
    has_row_above = r > 0
    main = jnp.where(last, right_hub, left_hub)
    is_main = c == main
    is_hub = (c == left_hub) | (c == right_hub)
    on_left = c <= left_hub
    low = jnp.where(on_left, 0, right_hub)
    high = jnp.where(on_left, left_hub, cols - 1)
    nxt = jnp.where(c < main, c + 1, c - 1)
    takes_left = c <= main
    takes_right = c >= main

    def dev(row, col, ind):
        return {"row": row, "col": col, "ind": ind}

    def remote(src, dst, send, recv, target):
        return pltpu.make_async_remote_copy(
            src_ref=src, dst_ref=dst, send_sem=send, recv_sem=recv,
            device_id=target, device_id_type=MESH)

    def when(cond, fn):
        pl.when(cond)(fn)

    def loop(lo, hi, fn):
        def body(step, carry):
            fn(step)
            return carry
        lax.fori_loop(lo, hi, body, 0)

    barrier = pltpu.get_barrier_semaphore()

    def greet(row, col, ind):
        pl.semaphore_signal(barrier, inc=1, device_id=dev(row, col, ind), device_id_type=MESH)

    when(c > 0, lambda: greet(r, c - 1, i))
    when(c + 1 < cols, lambda: greet(r, c + 1, i))
    when(has_row_below, lambda: greet(r + 1, c, i))
    when(has_row_above, lambda: greet(r - 1, c, i))
    for k in range(1, inds):
        greet(r, c, lax.rem(i + k, inds))
    load_x = pltpu.make_async_copy(x_ref, xs.at[c], load_sem.at[0])
    load_x.start()
    load_a = pltpu.make_async_copy(a_ref, am.at[0, c], load_sem.at[1])
    load_a.start()
    near = [c > 0, c + 1 < cols, has_row_below, has_row_above]
    pl.semaphore_wait(barrier, inds - 1 + sum(n.astype(jnp.int32) for n in near))

    pieces = 4
    piece = x_ref.shape[0] // pieces

    def send_x(col, src, h):
        at = pl.ds(h * piece, piece)
        return remote(src.at[at], xs.at[col, at], xsend.at[col, h], xrecv.at[col, h],
                      dev(r, nxt, i))

    def send_w(col, src):
        return remote(src, wl.at[col], wsend.at[col], wrecv.at[col], dev(r, nxt, i))

    def send_n(col, src):
        slot = col - low
        return remote(src, xn.at[slot], nsend.at[slot], nrecv.at[slot], dev(r - 1, c, i))

    def a_up(col, src):
        return remote(src, am.at[0, col], aup.at[col], arecv.at[col], dev(r, c + 1, i))

    def a_down(col, src):
        return remote(src, am.at[0, col], adn.at[col], arecv.at[col], dev(r, c - 1, i))

    def a_cross(col, row):
        return remote(am.at[0, col], am.at[1, col], axs.at[col], crecv.at[col], dev(row, c, i))

    def gives_n(col):
        return has_row_above & is_hub & (col >= low) & (col <= high) & (col < cols - 1)

    when(c + 1 < cols, lambda: a_up(c, a_ref).start())
    when(c > 0, lambda: a_down(c, a_ref).start())
    for h in range(pieces):
        when(~is_main, lambda h=h: send_x(c, x_ref, h).start())
    when(~is_main, lambda: send_w(c, w_ref).start())
    when(gives_n(c), lambda: send_n(c, x_ref).start())
    wl[c] = w_ref[...]

    def valid(kind, p, q):
        if kind:
            return has_row_below & (p < q) & ((q >= low) | is_main)
        return jnp.where(last, p >= q, p <= q) & (is_main | ((q >= low) & (q <= high)))

    def away(col):
        return jnp.abs(col - c)

    def ready(kind, p, q):
        return jnp.maximum(away(p) + kind, away(q))

    def reduce_send(kind, l, q, k):
        to = lax.rem(i + k, inds)
        return remote(gp.at[kind, l, q, to], rs.at[k - 1, kind, l, q], ssend.at[kind, l, q, 0, k],
                      rrecv.at[k - 1, kind, l, q], dev(r, c, to))

    def put_tile(kind, l, q):
        value = jnp.dot(xt[kind, l], xs[q], preferred_element_type=jnp.float32)
        gp[kind, l, q] = value.reshape(inds, part, tile)
        loop(1, inds, lambda k: reduce_send(kind, l, q, k).start())

    def use(col, before):
        def turn():
            l = col - low
            xt[0, l] = xs[col].T
            wide = jnp.broadcast_to(wl[col].astype(jnp.float32), (tile, tile))
            wc[l] = wide.T.astype(jnp.int32).reshape(inds, part, tile)

        mine = (col >= low) & (col <= high)
        when(mine, turn)

        def as_q(l):
            p = low + l
            when(((p == col) | before(p)) & (p <= high) & valid(0, p, col),
                 lambda: put_tile(0, l, col))
            when((away(p) + 1 <= away(col)) & (p <= high) & valid(1, p, col),
                 lambda: put_tile(1, l, col))

        loop(0, span, as_q)
        when(mine, lambda: loop(0, cols, lambda q: when(
            before(q) & valid(0, col, q), lambda: put_tile(0, col - low, q))))

    def use_next(col, step):
        l = col - low
        send_n(col, x_ref).wait_recv()
        xt[1, l] = xn[l].T
        loop(0, cols, lambda q: when(
            (away(q) < step) & valid(1, col, q), lambda: put_tile(1, l, q)))

    row_iota = lax.broadcasted_iota(jnp.int32, (part, tile), 0) + i * part
    lane_iota = lax.broadcasted_iota(jnp.int32, (part, tile), 1)

    def s_send(kind, l, q, which, k, row, col, slot):
        to = lax.rem(i + k, inds)
        return remote(sq.at[kind, l, q], sm.at[kind, slot, i], ssend.at[kind, l, q, which, k],
                      srecv.at[kind, slot, i], dev(row, col, to))

    def targets(kind, l, q, act, keep):
        p = low + l
        here = q == c

        def second():
            when(here, keep(q, p))
            first = here.astype(jnp.int32)
            loop(first, inds, lambda k: act(s_send(kind, l, q, 1, k, r, q, p)))

        def same_row():
            when(p == c, keep(p, q))
            first = (p == c).astype(jnp.int32)
            loop(first, inds, lambda k: act(s_send(kind, l, q, 0, k, r, p, q)))

        if kind:
            second()
            loop(0, inds, lambda k: act(s_send(kind, l, q, 0, k, r + 1, p, q)))
        else:
            when(p != q, second)
            same_row()

    def finish(kind, l, q):
        p = low + l
        total = gp[kind, l, q, i]
        for k in range(1, inds):
            reduce_send(kind, l, q, k).wait()
            total = total + rs[k - 1, kind, l, q]
        corr = total / samples
        rsq = corr * corr
        adj = rsq - (1.0 - rsq) / (samples - 2)
        by_lane = jnp.broadcast_to(wl[q], (part, tile))
        if kind:
            pos, lim = ((r + 1) * cols + p) * tile + row_iota, by_lane
        else:
            rows_first = ((p == q) & (lane_iota >= row_iota)) | ((p != q) & ~last)
            pos = jnp.where(rows_first, (r * cols + q) * tile + lane_iota,
                            (r * cols + p) * tile + row_iota)
            lim = jnp.where(rows_first, wc[l, i], by_lane)
        val = jnp.where(pos < lim, adj, 0.0).astype(jnp.bfloat16)
        sq[kind, l, q] = val

        def keep(me, slot):
            def store():
                sm[kind, slot, i] = val
            return store

        targets(kind, l, q, lambda copy: copy.start(), keep)

    def each_tile(fn):
        for kind in range(2):
            def by_l(l, kind=kind):
                def by_q(q):
                    p = low + l
                    when((p <= high) & valid(kind, p, q), lambda: fn(kind, l, q, ready(kind, p, q)))
                loop(0, cols, by_q)
            loop(0, span, by_l)

    def pass_a(s):
        def from_left():
            col = c - s
            a_up(col, am.at[0, col]).wait_recv()
            when(c + 1 < cols, lambda: a_up(col, am.at[0, col]).start())
            when(has_row_above, lambda: a_cross(col, r - 1).start())

        def from_right():
            col = c + s
            a_down(col, am.at[0, col]).wait_recv()
            when(c > 0, lambda: a_down(col, am.at[0, col]).start())
            when(has_row_below, lambda: a_cross(col, r + 1).start())

        when(c - s >= 0, from_left)
        when(c + s < cols, from_right)

    def arrive(col, before):
        for h in range(pieces):
            send_x(col, xs.at[col], h).wait_recv()
            when(~is_main, lambda h=h: send_x(col, xs.at[col], h).start())
        when(gives_n(col), lambda: send_n(col, xs.at[col]).start())
        send_w(col, wl.at[col]).wait_recv()
        when(~is_main, lambda: send_w(col, wl.at[col]).start())
        when(is_hub, lambda: use(col, before))

    def needs_n(col):
        return has_row_below & is_hub & (col >= low) & (col <= high) & (col < cols - 1)

    load_x.wait()
    when(is_hub, lambda: use(c, lambda x: x < 0))

    def step(s):
        left, right = c - s + 1, c + s - 1
        when((left >= 0) & needs_n(left), lambda: use_next(left, s))
        when((s > 1) & (right < cols) & needs_n(right), lambda: use_next(right, s))
        when(s < cols, lambda: pass_a(s))
        left, right = c - s, c + s
        when((left >= 0) & takes_left, lambda: arrive(left, lambda x: away(x) < s))
        when((right < cols) & takes_right, lambda: arrive(
            right, lambda x: (away(x) < s) | (x == c - s)))
        when(is_hub, lambda: each_tile(lambda kind, l, q, t: when(
            t == s - 1, lambda: finish(kind, l, q))))

    steps = span + 2
    loop(1, steps, step)
    when(is_hub, lambda: each_tile(lambda kind, l, q, t: when(
        t >= steps - 1, lambda: finish(kind, l, q))))
    loop(steps, cols, pass_a)

    load_a.wait()

    def take(kind, slot, q):
        remote(sq.at[0, 0, 0], sm.at[kind, slot, q], ssend.at[0, 0, 0, 0, 0],
               srecv.at[kind, slot, q], dev(r, c, lax.rem(i + 1, inds))).wait_recv()

    def take_all(kind, slot, p, same_row):
        home = jnp.where(p <= left_hub, left_hub, right_hub)
        first = (same_row & (home == c)).astype(jnp.int32)
        loop(first, inds, lambda k: take(kind, slot, lax.rem(i + k, inds)))

    def add(kind, slot, flip):
        lhs = am[kind, slot]
        rhs = sm[kind, slot].reshape(tile, tile)
        dims = (((1,), (1,)), ((), ())) if flip else (((1,), (0,)), ((), ()))
        o_ref[...] += lax.dot_general(lhs, rhs, dims, preferred_element_type=jnp.float32)

    o_ref[...] = jnp.zeros_like(o_ref)

    def add_row(col):
        p = jnp.where(last, jnp.maximum(c, col), jnp.minimum(c, col))
        take_all(0, col, p, c >= 0)
        when(p == c, lambda: add(0, col, True))
        when(p != c, lambda: add(0, col, False))

    loop(0, cols, add_row)

    def add_cross(col):
        remote(am.at[0, col], am.at[1, col], axs.at[col], crecv.at[col],
               dev(r, nxt, i)).wait_recv()
        take_all(1, col, jnp.minimum(c, col), col < c)
        when(col < c, lambda: add(1, col, False))
        when(col > c, lambda: add(1, col, True))

    when(has_row_below, lambda: loop(0, c, add_cross))
    when(has_row_above, lambda: loop(c + 1, cols, add_cross))

    def sent_x(col):
        for h in range(pieces):
            send_x(col, xs.at[col], h).wait_send()
        send_w(col, wl.at[col]).wait_send()

    when(c < main, lambda: loop(0, c + 1, sent_x))
    when(c > main, lambda: loop(c, cols, sent_x))
    loop(low, high + 1, lambda col: when(
        gives_n(col), lambda: send_n(col, xs.at[col]).wait_send()))
    when(c + 1 < cols, lambda: loop(0, c + 1, lambda q: a_up(q, am.at[0, q]).wait_send()))
    when(c > 0, lambda: loop(c, cols, lambda q: a_down(q, am.at[0, q]).wait_send()))
    when(has_row_above, lambda: loop(0, c, lambda q: a_cross(q, r - 1).wait_send()))
    when(has_row_below, lambda: loop(c + 1, cols, lambda q: a_cross(q, r + 1).wait_send()))

    def drain(kind, l, q, t):
        targets(kind, l, q, lambda copy: copy.wait_send(), lambda me, slot: lambda: None)

    when(is_hub, lambda: each_tile(drain))


def per_device(rows, cols, inds, dosages, annotations, window_end):
    depth, tile = dosages.shape
    ann = annotations.shape[0]
    samples = depth * inds
    part = tile // inds
    span = max(cols // 2, cols - cols // 2)
    dma = pltpu.SemaphoreType.DMA
    sems = (dma((2,)), dma((cols, 4)), dma((cols, 4)), dma((span,)), dma((span,)), dma((cols,)),
            dma((cols,)), dma((cols,)), dma((cols,)), dma((cols,)), dma((cols,)), dma((cols,)),
            dma((inds - 1, 2, span, cols)),
            dma((2, span, cols, 2, inds)), dma((2, cols, inds)))
    return pl.pallas_call(
        functools.partial(kernel, rows, cols, inds, samples),
        out_shape=jax.ShapeDtypeStruct((ann, tile), jnp.float32),
        in_specs=[pl.BlockSpec(memory_space=pl.ANY), pl.BlockSpec(memory_space=pl.ANY),
                  pl.BlockSpec(memory_space=pltpu.VMEM)],
        out_specs=pl.BlockSpec(memory_space=pltpu.VMEM),
        scratch_shapes=[
            pltpu.VMEM((cols, depth, tile), jnp.bfloat16),
            pltpu.VMEM((span, depth, tile), jnp.bfloat16),
            pltpu.VMEM((2, span, tile, depth), jnp.bfloat16),
            pltpu.VMEM((cols, 1, tile), jnp.int32),
            pltpu.VMEM((span, inds, part, tile), jnp.int32),
            pltpu.VMEM((2, span, cols, inds, part, tile), jnp.float32),
            pltpu.VMEM((inds - 1, 2, span, cols, part, tile), jnp.float32),
            pltpu.VMEM((2, span, cols, part, tile), jnp.bfloat16),
            pltpu.VMEM((2, cols, inds, part, tile), jnp.bfloat16),
            pltpu.VMEM((2, cols, ann, tile), jnp.bfloat16),
            sems,
        ],
        compiler_params=pltpu.CompilerParams(collective_id=0, has_side_effects=True),
    )(dosages, annotations, window_end.reshape(1, tile))


def solution(mesh):
    in_specs = (P("ind", ("row", "col")), P("ind", ("row", "col")), P(("row", "col")))
    out_specs = P("ind", ("row", "col"))
    body = functools.partial(per_device, mesh.shape["row"], mesh.shape["col"], mesh.shape["ind"])
    return jax.shard_map(body, mesh=mesh, in_specs=in_specs, out_specs=out_specs, check_vma=False)
```
